32 devices in a mesh: wide: 8 (over y, x, core), narrow: 4 (over z).
Axes of the slice: x: 2, y: 2, z: 4, core: 2. Of those that a mesh axis runs over, the one named last changes fastest.
Arguments:
- tokens: bfloat16 [3072, 5120], P('wide'), may hold values from -6 to 6
- norm_gain: float32 [5120], replicated, may hold values from 0.1 to 1.9
- w_query: bfloat16 [5120, 5120], P('wide', 'narrow'), may hold values from -0.078125 to 0.078125
- w_keyval: bfloat16 [5120, 2, 1024], P('wide', None, 'narrow'), may hold values from -0.078125 to 0.078125
- w_output: bfloat16 [5120, 5120], P('narrow', 'wide'), may hold values from -0.75 to 0.75
- prompt_cache: bfloat16 [16, 2, 4096, 1024], P(None, None, 'wide', 'narrow'), may hold values from -64 to 64
- stretch_lengths: int32 [16], replicated, may hold values from 1 to 768, 3072 in all
- stretch_starts: int32 [16], replicated, may hold values from 0 to 2047
- page_route: int32 [8, 16], P('wide'), may hold values from 0 to 15, each once within a row
Outputs:
- attn_out: bfloat16 [3072, 5120], P('wide', 'narrow')
- decode_layout_cache: bfloat16 [4, 8, 2, 128, 32, 512], P('narrow', None, None, 'wide')
The draws below stay inside these ranges and needn't reach their ends.
Inputs may be any that keep to these rules, and one draw needn't show every extreme that they name: `stretch_lengths`: stretches sum to 3072 tokens; the longest has exactly 768. `page_route`: each row is a permutation of 0 to 15.
All inputs are finite; a program needn't handle non-finite values.
Results may differ from the reference program's by a relative error of at most 0.017.
Values may be sent and summed in bfloat16 or wider, within the bound.
No kernel may reach another device: no remote copies, remote signals or barrier semaphores. Data moves between devices by JAX's collectives and lax.ppermute only.
A program may use at most 128 MiB of HBM per device.

```python
import math
import jax
import jax.numpy as jnp
import numpy as np
from jax import lax

D = 5120
QH = 40
KVH = 8
HEAD_SIZE = 128
RELAID_LAYERS = 16
PAGE_POSITIONS = 32
NREQ = 16
TOKENS = 3072
P_SIZE = 4096
PB = 16
PAGE_SLOTS = 128
GROUP_KEY_HEADS = 4
MOST = 768
N_WIDE = 8


def draw_prompt_cache(key, part):
    first = jax.random.fold_in(jax.random.fold_in(key, 7), 0)
    base = jax.random.normal(first, (RELAID_LAYERS, 2, P_SIZE, KVH * HEAD_SIZE), jnp.float32)
    return base.astype(jnp.bfloat16)


def plant(drawn, rng, smallest, top_value):
    spot = [jax.random.randint(jax.random.fold_in(rng, axis), (), 0, length) for axis, length in enumerate(drawn.shape)]
    longest = drawn.shape.index(max(drawn.shape))
    next_to = spot[:longest] + [(spot[longest] + 1) % drawn.shape[longest]] + spot[longest + 1:]
    return drawn.at[tuple(spot)].set(smallest).at[tuple(next_to)].set(top_value)


def block_scale(stream_key, extent, cuts, least, largest):
    level, own = 1.0, jax.random.fold_in(stream_key, 6)
    for position, shards_of in cuts:
        draws = jnp.exp(jax.random.uniform(jax.random.fold_in(own, position), (shards_of,), jnp.float32, least / len(cuts), largest / len(cuts)))
        level = level * jnp.repeat(draws, extent[position] // shards_of).reshape([-1 if axis == position else 1 for axis in range(len(extent))])
    return level


def split_up(count, total, bound, slope):
    loads = [(1 << 20) // math.isqrt(rank ** slope) + 1 for rank in range(2, count + 1)]
    spare, counts = total - bound - (count - 1), [1] * (count - 1)
    while spare > 0:
        candidates = [i for i in range(count - 1) if counts[i] < bound]
        pool, budget = sum([loads[i] for i in candidates]), spare
        for i in candidates:
            extra = min(bound - counts[i], max(1, budget * loads[i] // pool), spare)
            counts[i] = counts[i] + extra
            spare = spare - extra
    return np.array([bound] + counts)


def ragged_sizes(own_key, number_of, total, most, slope):
    if number_of == 2:
        one = jax.random.randint(own_key, (), max(1, total - most), min(most, total - 1) + 1)
        return jnp.stack([one, total - one])
    sizes = jnp.asarray(split_up(number_of, total, most, slope), jnp.int32)
    twos = (number_of - 1) // 2
    source_of, sink = sizes[1:1 + 2 * twos:2], sizes[2:2 + 2 * twos:2]
    margin = jnp.minimum(source_of - 1, most - sink)
    moved = jax.random.randint(jax.random.fold_in(own_key, 1), (twos,), 0, 1 << 20) % (margin + 1)
    sizes = sizes.at[1:1 + 2 * twos:2].set(source_of - moved).at[2:2 + 2 * twos:2].set(sink + moved)
    return sizes[jax.random.permutation(jax.random.fold_in(own_key, 2), number_of)]


def noise(own_key, shape, spread, most, cuts=(), kind=jnp.bfloat16):
    array = jax.random.normal(own_key, shape, jnp.float32) * spread
    if len(cuts) > 0:
        array = block_scale(own_key, shape, cuts, -0.22, 0.18) * array
    return jnp.clip(array, min=-most, max=most).astype(kind)


def setup_inputs(seed: int = 0) -> dict:
    seeds = jax.random.split(jax.random.key(seed), 10)
    tokens = noise(seeds[0], (TOKENS, D), 1.0, 6.0, ((0, 8),))
    norm_gain = jnp.clip(1.0 + 0.18 * jax.random.normal(seeds[1], (D,), jnp.float32), 0.1, 1.9)
    w_query = noise(seeds[2], (D, QH * HEAD_SIZE), D ** -0.5, 0.078125, ((0, 8), (1, 4)))
    w_keyval = noise(seeds[3], (D, 2, KVH * HEAD_SIZE), D ** -0.5, 0.078125, ((0, 8), (2, 4)))
    w_output = noise(seeds[4], (QH * HEAD_SIZE, D), 64 ** -0.5, 0.75, ((0, 4), (1, 8)))
    prompt_cache = draw_prompt_cache(jax.random.fold_in(seeds[9], 71), 0)
    stretch_lengths = ragged_sizes(seeds[6], NREQ, TOKENS, MOST, 2).astype(jnp.int32)
    stretch_starts = plant(jax.random.randint(seeds[7], (NREQ,), 0, 2048), jax.random.fold_in(seeds[7], 1), 0, 2047).astype(jnp.int32)
    page_route = jax.vmap(lambda own: jax.random.permutation(own, PB))(jax.random.split(seeds[8], N_WIDE)).reshape((N_WIDE, PB)).astype(jnp.int32)
    return dict(tokens=tokens, norm_gain=norm_gain, w_query=w_query, w_keyval=w_keyval, w_output=w_output, prompt_cache=prompt_cache, stretch_lengths=stretch_lengths, stretch_starts=stretch_starts, page_route=page_route)


def rotate(heads, positions):
    half = HEAD_SIZE // 2
    freq = 1000000.0 ** (-jnp.arange(half, dtype=jnp.float32) * 2.0 / HEAD_SIZE)
    angle = positions.astype(jnp.float32)[:, None] * freq[None, :]
    cosine = jnp.cos(angle)[:, None, :]
    sine = jnp.sin(angle)[:, None, :]
    first = heads[..., :half]
    second = heads[..., half:]
    return jnp.concatenate([first * cosine - second * sine, second * cosine + first * sine], -1)

def reference(tokens, norm_gain, w_query, w_keyval, w_output, prompt_cache, stretch_lengths, stretch_starts, page_route):
    xfull = tokens.astype(jnp.float32)
    normed = (xfull * lax.rsqrt(lax.optimization_barrier(jnp.mean(xfull * xfull, -1, keepdims=True)) + 1e-06) * norm_gain).astype(jnp.bfloat16)
    query = jnp.dot(normed, w_query, preferred_element_type=jnp.float32)
    keyval = jnp.dot(normed, w_keyval.reshape(D, 2 * KVH * HEAD_SIZE), preferred_element_type=jnp.float32).reshape(TOKENS, 2, KVH, HEAD_SIZE)
    ends = jnp.cumsum(stretch_lengths).astype(jnp.int32)
    begins = ends - stretch_lengths
    tok_index = jnp.arange(TOKENS, dtype=jnp.int32)
    seg = lax.optimization_barrier(jnp.sum((ends[None, :] <= tok_index[:, None]).astype(jnp.int32), 1)).astype(jnp.int32)
    pos = P_SIZE + stretch_starts[seg] + tok_index - begins[seg]
    rq = rotate(query.reshape(TOKENS, QH, HEAD_SIZE), pos).astype(jnp.bfloat16)
    rk = rotate(keyval[:, 0], pos).astype(jnp.bfloat16)
    rv = keyval[:, 1].astype(jnp.bfloat16)
    keys = jnp.concatenate([prompt_cache[0, 0].reshape(P_SIZE, KVH, HEAD_SIZE), rk], 0).astype(jnp.float32)
    vals = jnp.concatenate([prompt_cache[0, 1].reshape(P_SIZE, KVH, HEAD_SIZE), rv], 0).astype(jnp.float32)
    key_seg = jnp.concatenate([jnp.full((P_SIZE,), -1, jnp.int32), seg])
    key_tok = jnp.concatenate([jnp.zeros((P_SIZE,), jnp.int32), tok_index])
    group = QH // KVH
    qblock = math.gcd(TOKENS, 128)
    scale = HEAD_SIZE ** (-0.5)

    def one_block(index):
        first = index * qblock
        qpart = lax.dynamic_slice_in_dim(rq, first, qblock, 0).reshape(qblock, KVH, group, HEAD_SIZE).astype(jnp.float32)
        sseg = lax.dynamic_slice_in_dim(seg, first, qblock, 0)
        stok = lax.dynamic_slice_in_dim(tok_index, first, qblock, 0)
        score = jnp.einsum('tkgd,skd->kgts', qpart, keys) * scale
        visible = (key_seg[None, :] < 0) | (key_seg[None, :] == sseg[:, None]) & (key_tok[None, :] <= stok[:, None])
        masked = jnp.where(visible, score, -jnp.inf)
        top = lax.optimization_barrier(jnp.max(masked, -1, keepdims=True))
        ework = jnp.where(visible, jnp.exp(masked - top), 0.0)
        den = lax.optimization_barrier(jnp.sum(ework, -1))
        ebf = lax.optimization_barrier(ework.astype(jnp.bfloat16)).astype(jnp.float32)
        weighted = jnp.einsum('kgts,skd->kgtd', ebf, vals) / den[..., None]
        return jnp.transpose(weighted, (2, 0, 1, 3)).reshape(qblock, QH * HEAD_SIZE).astype(jnp.bfloat16)
    attn = lax.map(one_block, jnp.arange(TOKENS // qblock, dtype=jnp.int32)).reshape(TOKENS, QH * HEAD_SIZE)
    attn_out = jnp.dot(attn, w_output, preferred_element_type=jnp.float32).astype(jnp.bfloat16)
    pages = prompt_cache.reshape(RELAID_LAYERS, 2, N_WIDE, PB, PAGE_POSITIONS, KVH * HEAD_SIZE)
    inverse = jnp.argsort(page_route, axis=1).astype(jnp.int32)
    page_slots = jnp.arange(PAGE_SLOTS, dtype=jnp.int32)
    slot_block = page_slots % N_WIDE
    slot_rank = page_slots // N_WIDE
    chosen_pages = pages[:, :, slot_block, inverse[slot_block, slot_rank]]
    head_groups = KVH // GROUP_KEY_HEADS
    arranged_pages = chosen_pages.reshape(2, RELAID_LAYERS // 2, 2, PAGE_SLOTS, PAGE_POSITIONS, head_groups, GROUP_KEY_HEADS * HEAD_SIZE)
    decode_layout_cache = jnp.transpose(arranged_pages, (5, 0, 1, 2, 3, 4, 6)).reshape(2 * head_groups, RELAID_LAYERS // 2, 2, PAGE_SLOTS, PAGE_POSITIONS, GROUP_KEY_HEADS * HEAD_SIZE)
    return (attn_out, decode_layout_cache)
```

```python
import functools
import math

import jax
import jax.numpy as jnp
from jax import lax
from jax.experimental import pallas as pl
from jax.experimental.pallas import tpu as pltpu
from jax.sharding import PartitionSpec as P

HEAD_SIZE = 128
F32 = jnp.float32
BF16 = jnp.bfloat16
ANY = pl.BlockSpec(memory_space=pl.ANY)
SMEM = pl.BlockSpec(memory_space=pltpu.SMEM)
VMEM = pl.BlockSpec(memory_space=pltpu.VMEM)
DMA = pltpu.SemaphoreType.DMA
BIG = 60 * 1024 * 1024


def sds(shape, dtype=BF16):
    return jax.ShapeDtypeStruct(shape, dtype)


def cost(flops, moved):
    return pl.CostEstimate(flops=int(flops), bytes_accessed=int(moved), transcendentals=0)


def from_partner(value, axis, stride):
    mask = 2**stride
    pairs = [(source, source ^ mask) for source in range(lax.axis_size(axis))]
    return lax.ppermute(value, axis, pairs)


def rotate(heads, positions):
    half = heads.shape[-1] // 2
    freq = 1000000.0 ** (-jnp.arange(half, dtype=jnp.float32) * 2.0 / heads.shape[-1])
    angle = positions.astype(jnp.float32)[:, None] * freq[None, :]
    cosine = jnp.cos(angle)[:, None, :]
    sine = jnp.sin(angle)[:, None, :]
    first = heads[..., :half]
    second = heads[..., half:]
    return jnp.concatenate([first * cosine - second * sine, second * cosine + first * sine], -1)


def segment_of(tok_ids, ends):
    return jnp.sum((ends[None, :] <= tok_ids[:, None]).astype(jnp.int32), 1)


def relay_pages(prompt_cache, page_route):
    layers, kinds, cache_rows, channels = prompt_cache.shape
    per_block = page_route.shape[1]
    page_len = cache_rows // per_block
    pages = prompt_cache.reshape(layers, kinds, per_block, page_len, channels)
    inverse = (
        jnp.zeros((per_block,), jnp.int32)
        .at[page_route[0]]
        .set(jnp.arange(per_block, dtype=jnp.int32))
    )
    ordered = jnp.take(pages, inverse, axis=2)[:, :, :, None]
    moved = lax.all_to_all(ordered, "wide", split_axis=2, concat_axis=3, tiled=True)
    moved = moved.reshape(layers, kinds, per_block, page_len, channels)
    parity = lax.axis_index("narrow") % 2
    half = layers // 2
    keep = lax.dynamic_slice_in_dim(moved, parity * half, half, 0)
    outgoing = lax.dynamic_slice_in_dim(moved, (1 - parity) * half, half, 0)
    partner = from_partner(outgoing, "narrow", 0)
    joined = jnp.where(
        parity == 0, jnp.concatenate([keep, partner], -1), jnp.concatenate([partner, keep], -1)
    )
    return joined[None]


def on_device_plain(
    tokens,
    norm_gain,
    w_query,
    w_keyval,
    w_output,
    prompt_cache,
    stretch_lengths,
    stretch_starts,
    page_route,
):
    decode_layout_cache = relay_pages(prompt_cache, page_route)
    tok_rows = tokens.shape[0]
    cache_rows = prompt_cache.shape[2]
    channels = prompt_cache.shape[3]
    head_dim = HEAD_SIZE
    kv_local = channels // head_dim
    q_cols = w_query.shape[1]
    q_local = q_cols // head_dim
    group = q_local // kv_local
    xfull = tokens.astype(jnp.float32)
    normed = (
        xfull * lax.rsqrt(jnp.mean(xfull * xfull, -1, keepdims=True) + 1e-06) * norm_gain
    ).astype(jnp.bfloat16)
    piece_q = lax.all_gather(w_query, "wide", axis=0, tiled=True)
    piece_kv = lax.all_gather(w_keyval, "wide", axis=0, tiled=True)
    rows = piece_q.shape[0]
    query = jnp.dot(normed, piece_q, preferred_element_type=jnp.float32)
    keyval = jnp.dot(
        normed, piece_kv.reshape(rows, 2 * channels), preferred_element_type=jnp.float32
    )
    keyval = keyval.reshape(tok_rows, 2, kv_local, head_dim)
    ends = jnp.cumsum(stretch_lengths)
    begins = ends - stretch_lengths
    tok_ids = lax.axis_index("wide") * tok_rows + jnp.arange(tok_rows, dtype=jnp.int32)
    seg = segment_of(tok_ids, ends)
    prompt_len = cache_rows * lax.axis_size("wide")
    onehot = (
        seg[:, None] == jnp.arange(stretch_lengths.shape[0], dtype=jnp.int32)[None, :]
    ).astype(jnp.int32)
    pos = prompt_len + jnp.sum(onehot * (stretch_starts - begins)[None, :], 1) + tok_ids
    rq = rotate(query.reshape(tok_rows, q_local, head_dim), pos).astype(jnp.bfloat16)
    rk = rotate(keyval[:, 0], pos).astype(jnp.bfloat16)
    rv = keyval[:, 1].astype(jnp.bfloat16)
    newblock = jnp.stack([rk.reshape(tok_rows, channels), rv.reshape(tok_rows, channels)], 0)
    keyblock = jnp.concatenate([prompt_cache[0], newblock], 1)
    span = cache_rows + tok_rows
    qgroup = rq.reshape(tok_rows, kv_local, group, head_dim)
    scale = head_dim ** (-0.5)

    def attend_block(carry, piece, start):
        top, den, acc = carry
        rows = piece.shape[1]
        index = start + jnp.arange(rows, dtype=jnp.int32)
        owner = index // span
        local = index % span
        is_prompt = local < cache_rows
        key_tok = owner * tok_rows + local - cache_rows
        key_seg = segment_of(key_tok, ends)
        keys = piece[0].reshape(rows, kv_local, head_dim)
        vals = piece[1].reshape(rows, kv_local, head_dim)
        score = (
            jnp.einsum("tkgd,skd->kgts", qgroup, keys, preferred_element_type=jnp.float32) * scale
        )
        visible = is_prompt[None, :] | (key_seg[None, :] == seg[:, None]) & (
            key_tok[None, :] <= tok_ids[:, None]
        )
        score = jnp.where(visible, score, -1e30)
        new_top = jnp.maximum(top, jnp.max(score, -1))
        factor = jnp.exp(top - new_top)
        weights = jnp.where(visible, jnp.exp(score - new_top[..., None]), 0.0)
        den = den * factor + jnp.sum(weights, -1)
        acc = acc * factor[..., None] + jnp.einsum(
            "kgts,skd->kgtd", weights.astype(jnp.bfloat16), vals, preferred_element_type=jnp.float32
        )
        return (new_top, den, acc)

    carry = (
        jnp.full((kv_local, group, tok_rows), -1e30, jnp.float32),
        jnp.zeros((kv_local, group, tok_rows), jnp.float32),
        jnp.zeros((kv_local, group, tok_rows, head_dim), jnp.float32),
    )
    piece = lax.all_gather(keyblock, "wide", axis=1, tiled=True)
    rows = piece.shape[1]
    count = rows // span
    parts = jnp.transpose(piece.reshape(2, count, span, channels), (1, 0, 2, 3))

    def step(inner, item):
        number, part_piece = item
        return (attend_block(inner, part_piece, number * span), None)

    carry, unused = lax.scan(step, carry, (jnp.arange(count, dtype=jnp.int32), parts))
    top, den, acc = carry
    attn = (
        jnp.transpose(acc / den[..., None], (2, 0, 1, 3))
        .reshape(tok_rows, q_cols)
        .astype(jnp.bfloat16)
    )
    partial_out = jnp.dot(
        attn,
        lax.all_gather(w_output, "wide", axis=1, tiled=True),
        preferred_element_type=jnp.float32,
    )
    attn_out = lax.psum_scatter(
        partial_out.astype(jnp.bfloat16), "narrow", scatter_dimension=1, tiled=True
    )
    return (attn_out, decode_layout_cache)


def wide_xor(value, mask):
    return lax.ppermute(value, "wide", [(i, i ^ mask) for i in range(lax.axis_size("wide"))])


def both_xor(value, wide_mask, narrow_mask):
    wide, narrow = lax.axis_size("wide"), lax.axis_size("narrow")
    pairs = [
        (w * narrow + n, (w ^ wide_mask) * narrow + (n ^ narrow_mask))
        for w in range(wide)
        for n in range(narrow)
    ]
    return lax.ppermute(value, ("wide", "narrow"), pairs)


def after(value, *others):
    return lax.optimization_barrier((value,) + others)[0]


def gather_plane(first, second, waits=()):
    if waits:
        first = after(first, *waits)
        second = after(second, *waits)
    got = {0: first, 1: second}
    got[2] = wide_xor(first, 2)
    got[5] = wide_xor(second, 4)
    got[4] = wide_xor(first, 4)
    got[3] = wide_xor(second, 2)
    got[6] = wide_xor(got[2], 4)
    got[7] = wide_xor(got[5], 2)
    return got


def prep_kernel(meta, wq, wkv, cache, mine, send, kv_mine, kv_send, sem):
    core = lax.rem(meta[0], 2)
    copies = []
    width = wq.shape[1] // 2

    def lanes(start, size):
        return pl.ds(pl.multiple_of(start, HEAD_SIZE), size)

    number = 0
    for out, kv_out, head in ((send, kv_send, 1 - core), (mine, kv_mine, core)):
        copies += [
            pltpu.make_async_copy(
                wq.at[:, lanes(head * width, width)], out.at[:, 0:width], sem.at[number]
            ),
            pltpu.make_async_copy(
                wkv.at[:, lanes(head * HEAD_SIZE, HEAD_SIZE)],
                out.at[:, width : width + HEAD_SIZE],
                sem.at[number + 1],
            ),
            pltpu.make_async_copy(
                wkv.at[:, lanes((2 + head) * HEAD_SIZE, HEAD_SIZE)],
                out.at[:, width + HEAD_SIZE : width + 2 * HEAD_SIZE],
                sem.at[number + 2],
            ),
            pltpu.make_async_copy(
                cache.at[0, :, :, lanes(head * HEAD_SIZE, HEAD_SIZE)], kv_out, sem.at[number + 3]
            ),
        ]
        number += 4
    for copy in copies:
        copy.start()
    for copy in copies:
        copy.wait()


def norm_kernel(x, gain, out):
    value = x[...].astype(F32)
    mean = jnp.mean(value * value, -1, keepdims=True)
    out[...] = (value * lax.rsqrt(mean + 1e-06) * gain[...]).astype(BF16)


def project_kernel(keys, last, meta, *refs):
    count = len(keys)
    x_own, x_other = refs[:2]
    pieces = refs[2 : 2 + count]
    rest = refs[2 + count :]
    if last:
        start, cosine, sine, rq, kv, xbuf, wbuf, acc, xsem, wsem = rest
    else:
        acc, xbuf, wbuf, xsem, wsem = rest
    rows = x_own.shape[0]
    depth = xbuf.shape[2]
    copies = []
    for i, key in enumerate(keys):
        block = jnp.bitwise_xor(meta[0], key)
        columns = pl.ds(pl.multiple_of(block * depth, HEAD_SIZE), depth)
        group = [
            pltpu.make_async_copy(x_own.at[:, columns], xbuf.at[i, 0:rows], xsem.at[2 * i]),
            pltpu.make_async_copy(
                x_other.at[:, columns], xbuf.at[i, rows : 2 * rows], xsem.at[2 * i + 1]
            ),
            pltpu.make_async_copy(pieces[i], wbuf.at[i], wsem.at[i]),
        ]
        for copy in group:
            copy.start()
        copies.append(group)
    tile = 256
    for i in range(count):
        for copy in copies[i]:
            copy.wait()

        def step(number, unused, i=i):
            at = pl.ds(pl.multiple_of(number * tile, tile), tile)
            part = jnp.dot(xbuf[i, at, :], wbuf[i], preferred_element_type=F32)
            if i == 0:
                acc[at, :] = start[at, :] + part if last else part
            else:
                acc[at, :] = acc[at, :] + part
            return unused

        lax.fori_loop(0, 2 * rows // tile, step, 0)
    if last:
        heads = rq.shape[1] // HEAD_SIZE

        def turn(number, unused):
            at = pl.ds(pl.multiple_of(number * 128, 128), 128)
            c, s = cosine[at, :], sine[at, :]
            for h in range(heads + 1):
                value = acc[at, h * HEAD_SIZE : (h + 1) * HEAD_SIZE]
                turned = (value * c + pltpu.roll(value, HEAD_SIZE // 2, 1) * s).astype(BF16)
                if h < heads:
                    rq[at, h * HEAD_SIZE : (h + 1) * HEAD_SIZE] = turned
                else:
                    kv[0, at, :] = turned
            kv[1, at, :] = acc[at, (heads + 1) * HEAD_SIZE :].astype(BF16)
            return unused

        lax.fori_loop(0, 2 * rows // 128, turn, 0)


def project(keys, meta, x_own, x_other, pieces, more=None):
    rows = 2 * x_own.shape[0]
    depth, width = pieces[0].shape
    count = len(keys)
    last = more is not None
    heads = width // HEAD_SIZE - 2
    scratch = [
        pltpu.VMEM((count, rows, depth), BF16),
        pltpu.VMEM((count, depth, width), BF16),
    ]
    if last:
        scratch.append(pltpu.VMEM((rows, width), F32))
        out = (sds((rows, heads * HEAD_SIZE)), sds((2, rows, HEAD_SIZE)))
        extra = list(more)
    else:
        out = sds((rows, width), F32)
        extra = []
    return pl.pallas_call(
        functools.partial(project_kernel, keys, last),
        out_shape=out,
        in_specs=[SMEM] + [ANY] * (2 + count) + [VMEM] * len(extra),
        out_specs=(VMEM, VMEM) if last else VMEM,
        scratch_shapes=scratch + [DMA((2 * count,)), DMA((count,))],
        compiler_params=pltpu.CompilerParams(vmem_limit_bytes=BIG),
        cost_estimate=cost(2 * count * rows * depth * width, 2 * count * (rows + width) * depth),
        name="project",
    )(meta, x_own, x_other, *pieces, *extra)


def attend_kernel(
    count, block, chunk, span, half, meta, ends, rq, kv, prev, *refs
):
    pieces = refs[:count]
    out, keys, vals, new_keys, new_vals, top, acc, sem = refs[count:]
    step = pl.program_id(0)
    rows_piece = pieces[0].shape[1]
    device = meta[0]
    core = lax.rem(device, 2)
    mine_block = jnp.bitwise_xor(device, step)
    base = (device - core - 2) * block
    sub = rq.shape[0]
    heads = rq.shape[1] // HEAD_SIZE

    @pl.when(step == 0)
    def _():
        copies = []
        for i in range(count):
            at = slice(i * rows_piece, (i + 1) * rows_piece)
            copies.append(pltpu.make_async_copy(pieces[i].at[0], keys.at[at], sem.at[2 * i]))
            copies.append(
                pltpu.make_async_copy(
                    pieces[i].at[1], vals.at[at, 0:HEAD_SIZE], sem.at[2 * i + 1]
                )
            )
        for copy in copies:
            copy.start()
        for source, place in ((prev, 0), (kv, 2 * block)):
            for half in range(2):
                where = place + (core if half == 0 else 1 - core) * block
                at = pl.ds(pl.multiple_of(where, 128), block)
                new_keys[at, :] = source[0, half * block : (half + 1) * block, :]
                new_vals[at, 0:HEAD_SIZE] = source[1, half * block : (half + 1) * block, :]
        vals[:, HEAD_SIZE:] = jnp.ones((vals.shape[0], HEAD_SIZE), BF16)
        new_vals[:, HEAD_SIZE:] = jnp.ones((new_vals.shape[0], HEAD_SIZE), BF16)
        for copy in copies:
            copy.wait()

    q = jnp.concatenate([rq[:, h * HEAD_SIZE : (h + 1) * HEAD_SIZE] for h in range(heads)], 0)
    factor = HEAD_SIZE**-0.5 * math.log2(math.e)

    def scores(part):
        return (
            lax.dot_general(q, part, (((1,), (1,)), ((), ())), preferred_element_type=F32) * factor
        )

    for i in range(count * rows_piece // chunk):
        at = slice(i * chunk, (i + 1) * chunk)
        score = scores(keys[at, :])
        high = jnp.max(score, -1, keepdims=True)
        if i == 0:
            e = jnp.exp2(score - high).astype(BF16)
            acc[...] = jnp.dot(e, vals[at, :], preferred_element_type=F32)
            top[...] = high
        else:
            old = top[...]
            new = jnp.maximum(old, high)
            e = jnp.exp2(score - new).astype(BF16)
            acc[...] = acc[...] * jnp.exp2(old - new) + jnp.dot(
                e, vals[at, :], preferred_element_type=F32
            )
            top[...] = new

    first = mine_block * block + half * sub

    def begin_of(tok):
        low = jnp.zeros_like(tok)
        for i in range(ends.shape[0]):
            low = jnp.maximum(low, jnp.where(ends[i] <= tok, ends[i], 0))
        return low

    tok = first + lax.broadcasted_iota(jnp.int32, (sub, 1), 0)
    low = begin_of(tok)
    toks = jnp.concatenate([tok] * heads, 0)
    lows = jnp.concatenate([low] * heads, 0)

    def visit(number, unused):
        at = pl.ds(pl.multiple_of(number * span, span), span)
        score = scores(new_keys[at, :])
        ids = base + number * span + lax.broadcasted_iota(jnp.int32, (1, span), 1)
        seen = (ids >= lows) & (ids <= toks)
        score = jnp.where(seen, score, -1e30)
        old = top[...]
        new = jnp.maximum(old, jnp.max(score, -1, keepdims=True))
        e = jnp.where(seen, jnp.exp2(score - new), 0.0).astype(BF16)
        acc[...] = acc[...] * jnp.exp2(old - new) + jnp.dot(
            e, new_vals[at, :], preferred_element_type=F32
        )
        top[...] = new
        return unused

    low_first = begin_of(first)
    lax.fori_loop(
        lax.div(low_first - base, span), lax.div(first + sub - 1 - base, span) + 1, visit, 0
    )
    for h in range(heads):
        at = slice(h * sub, (h + 1) * sub)
        out[:, h * HEAD_SIZE : (h + 1) * HEAD_SIZE] = (
            acc[at, 0:HEAD_SIZE] / acc[at, HEAD_SIZE:]
        ).astype(BF16)


def attend(meta, ends, rq, kv, prev, pieces, half):
    rows, width = rq.shape
    block = rows // 2
    sub = block // 2
    heads = width // HEAD_SIZE
    count = len(pieces)
    prompt = count * pieces[0].shape[1]
    chunk, span = 1024, 256
    whole = pl.BlockSpec(kv.shape, lambda i: (0, 0, 0))
    return pl.pallas_call(
        functools.partial(attend_kernel, count, block, chunk, span, half),
        out_shape=sds((block, width)),
        grid=(2,),
        in_specs=[SMEM, SMEM, pl.BlockSpec((sub, width), lambda i: (2 * i + half, 0)), whole, whole]
        + [ANY] * count,
        out_specs=pl.BlockSpec((sub, width), lambda i: (i, 0)),
        scratch_shapes=[
            pltpu.VMEM((prompt, HEAD_SIZE), BF16),
            pltpu.VMEM((prompt, 2 * HEAD_SIZE), BF16),
            pltpu.VMEM((2 * rows, HEAD_SIZE), BF16),
            pltpu.VMEM((2 * rows, 2 * HEAD_SIZE), BF16),
            pltpu.VMEM((heads * sub, 1), F32),
            pltpu.VMEM((heads * sub, 2 * HEAD_SIZE), F32),
            DMA((2 * count,)),
        ],
        compiler_params=pltpu.CompilerParams(vmem_limit_bytes=BIG),
        cost_estimate=cost(8 * block * width * prompt, 4 * prompt * HEAD_SIZE),
        name="attend",
    )(meta, ends, rq, kv, prev, *pieces)


def output_kernel(meta, mine, partner, *refs):
    tops, lows = refs[:4], refs[4:8]
    ours, theirs = refs[8:12], refs[12:16]
    buf, sem = refs[16:]
    rows = ours[0].shape[0]
    core = lax.rem(meta[0], 2)
    turn = jnp.bitwise_xor(lax.div(meta[0], 2), meta[1])
    for m in range(4):
        source = jnp.bitwise_xor(turn, m)
        for j in range(4):

            @pl.when(source == j)
            def _(m=m, j=j):
                pltpu.make_async_copy(tops[j], buf.at[m, 0], sem.at[2 * m]).start()
                pltpu.make_async_copy(lows[j], buf.at[m, 1], sem.at[2 * m + 1]).start()

    own = mine[...]
    got = jnp.concatenate([partner[rows:, :], partner[:rows, :]], 0)
    even = jnp.where(core == 0, own, got)
    odd = jnp.where(core == 0, got, own)
    for m in range(4):
        pltpu.make_async_copy(tops[0], buf.at[m, 0], sem.at[2 * m]).wait()
        pltpu.make_async_copy(lows[0], buf.at[m, 1], sem.at[2 * m + 1]).wait()
        value = (
            jnp.dot(even, buf[m, 0], preferred_element_type=F32)
            + jnp.dot(odd, buf[m, 1], preferred_element_type=F32)
        ).astype(BF16)
        ours[m][...] = value[:rows]
        theirs[m][...] = value[rows:]


def output_pieces(meta, mine, partner, weights):
    rows, depth = mine.shape
    width = weights[0].shape[1]
    return pl.pallas_call(
        output_kernel,
        out_shape=(sds((rows // 2, width)),) * 8,
        in_specs=[SMEM, VMEM, VMEM] + [ANY] * 8,
        out_specs=(VMEM,) * 8,
        scratch_shapes=[pltpu.VMEM((4, 2, depth, width), BF16), DMA((8,))],
        compiler_params=pltpu.CompilerParams(vmem_limit_bytes=BIG),
        cost_estimate=cost(16 * rows * depth * width, 16 * depth * width),
        name="output_pieces",
    )(meta, mine, partner, *[weights[k] for k in (0, 2, 4, 6)], *[weights[k] for k in (1, 3, 5, 7)])


def total_kernel(meta, *refs):
    out = refs[16]
    rows, width = refs[0].shape
    core = lax.rem(meta[0], 2)
    for i in range(4):
        value = sum(ref[...].astype(F32) for ref in refs[4 * i : 4 * i + 4]).astype(BF16)
        side = 1 - core if i % 2 else core
        at = slice(i // 2 * rows, (i // 2 + 1) * rows)
        out[at, pl.ds(pl.multiple_of(side * width, HEAD_SIZE), width)] = value


def pack_kernel(meta, route, cache, partner, *refs):
    outs = refs[:8]
    buf, own_sem, got_sem, out_sem = refs[8:]
    half = partner.shape[0]
    page = buf.shape[4]
    width = partner.shape[3]
    pages = route.shape[1]
    parity = lax.rem(meta[1], 2)
    copies = []
    for t in range(pages):
        rank = route[0, t]
        key = jnp.bitwise_xor(lax.div(rank, 2), meta[0])
        slot = lax.rem(rank, 2)
        at = slice(t * page, (t + 1) * page)
        copies.append(
            pltpu.make_async_copy(
                cache.at[pl.ds(parity * half, half), :, at, :],
                buf.at[key, :, :, slot, :, pl.ds(pl.multiple_of(parity * width, 128), width)],
                own_sem.at[t],
            )
        )
        copies.append(
            pltpu.make_async_copy(
                partner.at[:, :, at, :],
                buf.at[key, :, :, slot, :, pl.ds(pl.multiple_of((1 - parity) * width, 128), width)],
                got_sem.at[t],
            )
        )
    for copy in copies:
        copy.start()
    for copy in copies:
        copy.wait()
    copies = [pltpu.make_async_copy(buf.at[k], outs[k], out_sem.at[k]) for k in range(8)]
    for copy in copies:
        copy.start()
    for copy in copies:
        copy.wait()


def place_kernel(keys, aliased, meta, *refs):
    count = len(keys)
    pieces = refs[:count]
    out, buf, in_sem, out_sem = refs[count + (1 if aliased else 0) :]
    wide = 8
    ins = [pltpu.make_async_copy(pieces[i], buf.at[i], in_sem.at[i]) for i in range(count)]
    for copy in ins:
        copy.start()
    outs = []
    for i, key in enumerate(keys):
        ins[i].wait()
        source = jnp.bitwise_xor(meta[0], key)
        for s in range(2):
            copy = pltpu.make_async_copy(
                buf.at[i, :, :, s], out.at[0, :, :, s * wide + source], out_sem.at[2 * i + s]
            )
            copy.start()
            outs.append(copy)
    for copy in outs:
        copy.wait()


def place(keys, meta, pieces, into=None):
    half, kinds, two, page, width = pieces[0].shape
    count = len(keys)
    aliased = into is not None
    return pl.pallas_call(
        functools.partial(place_kernel, keys, aliased),
        out_shape=sds((1, half, kinds, 16, page, width)),
        in_specs=[SMEM] + [ANY] * (count + (1 if aliased else 0)),
        out_specs=ANY,
        scratch_shapes=[
            pltpu.VMEM((count, half, kinds, two, page, width), BF16),
            DMA((count,)),
            DMA((2 * count,)),
        ],
        input_output_aliases={count + 1: 0} if aliased else {},
        compiler_params=pltpu.CompilerParams(vmem_limit_bytes=BIG),
        cost_estimate=cost(0, 4 * count * half * kinds * two * page * width),
        name="place",
    )(meta, *pieces, *([into] if aliased else []))


def on_device(
    tokens,
    norm_gain,
    w_query,
    w_keyval,
    w_output,
    prompt_cache,
    stretch_lengths,
    stretch_starts,
    page_route,
):
    rows, model = tokens.shape
    layers, kinds, cache_rows, channels = prompt_cache.shape
    half = layers // 2
    wide = lax.axis_size("wide")
    device = lax.axis_index("wide").astype(jnp.int32)
    plane = lax.axis_index("narrow").astype(jnp.int32)
    meta = jnp.stack([device, plane])
    depth = w_query.shape[0]
    width = w_query.shape[1] // 2
    span = width + 2 * HEAD_SIZE

    mine, send, kv_mine, kv_send = pl.pallas_call(
        prep_kernel,
        out_shape=(
            sds((depth, span)),
            sds((depth, span)),
            sds((2, cache_rows, HEAD_SIZE)),
            sds((2, cache_rows, HEAD_SIZE)),
        ),
        in_specs=[SMEM, ANY, ANY, ANY],
        out_specs=(VMEM,) * 4,
        scratch_shapes=[DMA((8,))],
        compiler_params=pltpu.CompilerParams(vmem_limit_bytes=BIG),
        name="prep",
    )(meta, w_query, w_keyval.reshape(depth, 2 * channels), prompt_cache)
    weights = gather_plane(mine, wide_xor(send, 1))
    cached = gather_plane(kv_mine, wide_xor(kv_send, 1), [weights[k] for k in (2, 3, 4, 5)])
    out_rows = w_output.shape[0] // 2
    out_weights = gather_plane(
        w_output[:out_rows], w_output[out_rows:], [weights[k] for k in (6, 7)]
    )

    outgoing = lax.dynamic_slice_in_dim(prompt_cache, (1 - after(plane, mine) % 2) * half, half, 0)
    partner = from_partner(outgoing, "narrow", 0)

    sub = 128
    x_own = pl.pallas_call(
        norm_kernel,
        out_shape=sds((rows, model)),
        grid=(rows // sub,),
        in_specs=[
            pl.BlockSpec((sub, model), lambda i: (i, 0)),
            pl.BlockSpec((1, model), lambda i: (0, 0)),
        ],
        out_specs=pl.BlockSpec((sub, model), lambda i: (i, 0)),
        name="norm",
    )(tokens, norm_gain.reshape(1, model))
    x_other = wide_xor(x_own, 1)

    ends = jnp.cumsum(stretch_lengths).astype(jnp.int32)
    begins = ends - stretch_lengths
    within = jnp.arange(rows, dtype=jnp.int32)
    tok_ids = jnp.concatenate([device * rows + within, jnp.bitwise_xor(device, 1) * rows + within])
    seg = segment_of(tok_ids, ends)
    onehot = (
        seg[:, None] == jnp.arange(stretch_lengths.shape[0], dtype=jnp.int32)[None, :]
    ).astype(jnp.int32)
    pos = cache_rows * wide + jnp.sum(onehot * (stretch_starts - begins)[None, :], 1) + tok_ids
    pairs = HEAD_SIZE // 2
    freq = 1000000.0 ** (-jnp.arange(pairs, dtype=F32) * 2.0 / HEAD_SIZE)
    angle = pos.astype(F32)[:, None] * freq[None, :]
    cosine, sine = jnp.cos(angle), jnp.sin(angle)
    cosine = jnp.concatenate([cosine, cosine], -1)
    sine = jnp.concatenate([-sine, sine], -1)

    early, late = (0, 1, 2, 5, 4, 3), (6, 7)
    begun = project(early, meta, x_own, x_other, [weights[k] for k in early])
    rq, kv = project(
        late, meta, x_own, x_other, [weights[k] for k in late], (begun, cosine, sine)
    )
    prev = lax.ppermute(kv, "wide", [(i, i + 2) for i in range(wide - 2)])
    prompt = [cached[k] for k in range(8)]

    sums = []
    for half_block in range(2):
        done = attend(meta, ends, rq, kv, prev, prompt, half_block)
        results = output_pieces(meta, done, wide_xor(done, 1), out_weights)
        sums += [results[0]] + [both_xor(results[m], 0, m) for m in range(1, 4)]
        sums += [both_xor(results[4 + m], 1, m) for m in range(4)]
    out_width = w_output.shape[1]
    attn_out = pl.pallas_call(
        total_kernel,
        out_shape=sds((rows, 2 * out_width)),
        in_specs=[SMEM] + [VMEM] * 16,
        out_specs=VMEM,
        compiler_params=pltpu.CompilerParams(vmem_limit_bytes=BIG),
        name="total",
    )(meta, *sums)

    page = cache_rows // page_route.shape[1]
    packed = pl.pallas_call(
        pack_kernel,
        out_shape=(sds((half, kinds, 2, page, 2 * channels)),) * 8,
        in_specs=[SMEM, SMEM, ANY, ANY],
        out_specs=(ANY,) * 8,
        scratch_shapes=[
            pltpu.VMEM((8, half, kinds, 2, page, 2 * channels), BF16),
            DMA((16,)),
            DMA((16,)),
            DMA((8,)),
        ],
        compiler_params=pltpu.CompilerParams(vmem_limit_bytes=BIG),
        cost_estimate=cost(0, 4 * half * kinds * cache_rows * channels * 2),
        name="pack",
    )(meta, page_route, prompt_cache, partner)
    waits = {k: [out_weights[i] for i in ((2, 3, 4, 5) if k in (2, 4) else (6, 7))] for k in range(8)}
    moved = [packed[0], wide_xor(packed[1], 1)]
    moved += [wide_xor(after(packed[k], *waits[k]), k) for k in range(2, 8)]
    placed = place((0, 1, 2, 4), meta, [moved[k] for k in (0, 1, 2, 4)])
    placed = place((3, 5), meta, [moved[k] for k in (3, 5)], placed)
    placed = place((6, 7), meta, [moved[k] for k in (6, 7)], placed)
    return (attn_out, placed)


def solution(mesh):
    placed = (
        P("wide", None),
        P(),
        P("wide", "narrow"),
        P("wide", None, "narrow"),
        P("narrow", "wide"),
        P(None, None, "wide", "narrow"),
        P(),
        P(),
        P("wide", None),
    )
    fits = mesh.shape["wide"] == 8 and mesh.shape["narrow"] == 4
    return jax.shard_map(
        on_device if fits else on_device_plain,
        mesh=mesh,
        in_specs=placed,
        out_specs=(P("wide", "narrow"), P("narrow", None, None, "wide", None, None)),
        check_vma=False,
    )
```
